512 devices in a mesh: blk: 16 (over y_lo, x, core), grp: 32 (over z, y_hi).
Axes of the slice: x: 4, y: 4 (y_hi: 2, y_lo: 2; y = y_hi * 2 + y_lo), z: 16, core: 2. Of those that a mesh axis runs over, the one named last changes fastest.
Arguments:
- amps: bfloat16 [4096, 8, 512], P(('blk', 'grp')), may hold values from -6 to 6
- domains: int32 [4096, 8], replicated, may hold values from 0 to 15, all different within a row
- owner: int32 [4096], replicated, may hold values from 0 to 4095, as said below
- coupling: int32 [16, 16], replicated, may hold values from 0 to 1, as said below
- integrals: bfloat16 [8192, 8192], P('blk', 'grp'), may hold values from -0.125 to 0.125
Outputs:
- residual: float32 [4096, 8192], P('blk', 'grp')
The draws below stay inside these ranges and needn't reach their ends.
Inputs may be any that keep to these rules, and one draw needn't show every extreme that they name: `domains`: each row names 8 different pair blocks, and every block is named by some row. owner maps the occupied pairs of each group of 256 consecutive pairs one to one onto the slots of the same group. Every column of coupling holds exactly 8 ones.
All inputs are finite; a program needn't handle non-finite values.
Results may differ from the reference program's by a relative error of at most 0.0003.
Values may be sent and summed in bfloat16 or wider, within the bound.
No kernel may reach another device: no remote copies, remote signals or barrier semaphores. Data moves between devices by JAX's collectives and lax.ppermute only.
A program may use at most 64 MiB of HBM per device.

```python
import jax
import jax.numpy as jnp
from jax import lax

PB = 512
OP_GRP = 256
NVB = 16
NV = 8192
K = 8
OP = 4096


def draw_owner(key, part):
    n_groups = OP // OP_GRP
    group_keys = jax.random.split(key, n_groups)

    def shuffle_one(group_key):
        return jax.random.permutation(group_key, OP_GRP).astype(jnp.int32)
    shuffled = jax.vmap(shuffle_one)(group_keys)
    offsets = jnp.arange(n_groups, dtype=jnp.int32)[:, None] * OP_GRP
    return (shuffled + offsets).reshape(OP).astype(jnp.int32)


def draw_coupling(key, part):
    column_keys = jax.random.split(jax.random.fold_in(key, 7), NVB)

    def column_one(column_key):
        ranks = jax.random.permutation(column_key, NVB).astype(jnp.int32)
        return (ranks < NVB // 2).astype(jnp.int32)
    columns = jax.vmap(column_one)(column_keys)
    return jnp.transpose(columns).astype(jnp.int32)


def block_scale(own_key, shape, pieces, least, largest):
    def one(position, blocks):
        draws = jax.random.uniform(jax.random.fold_in(jax.random.fold_in(own_key, 6), position), (blocks,), jnp.float32, least / len(pieces), largest / len(pieces))
        return jnp.repeat(jnp.exp(draws), shape[position] // blocks).reshape((-1,) + (1,) * (len(shape) - position - 1))

    factor_of = one(*pieces[0])
    for cut in pieces[1:]:
        factor_of = factor_of * one(*cut)
    return factor_of


def picks_of(own_key, rows, amount, top, lift):
    sequence = jax.random.permutation(jax.random.fold_in(own_key, 1), amount)
    pull = sequence
    for power in range(3):
        pull = pull * pull // amount
    pull = pull * lift // amount
    tickets = jax.random.randint(jax.random.fold_in(own_key, 2), (rows, amount), 0, 4096) + pull
    fixed_rows = jax.random.permutation(jax.random.fold_in(own_key, 3), rows)[jnp.arange(amount) % rows]
    tickets = jnp.where(jnp.arange(rows)[:, None] == fixed_rows[None, :], 1 << 14, tickets)
    merit = tickets * amount + jnp.arange(amount)
    return lax.top_k(merit.astype(jnp.int32), top)[1].astype(jnp.int32)


def scatter_about(rng, shape, deviation, bound, shards=(), held_as=jnp.bfloat16):
    loudness = block_scale(rng, shape, shards, -0.22, 0.18) if shards else 1.0
    entries = jax.random.normal(rng, shape, jnp.float32) * deviation * loudness
    return jnp.minimum(jnp.maximum(entries, -bound), bound).astype(held_as)


def setup_inputs(seed: int = 0) -> dict:
    seeds = jax.random.split(jax.random.key(seed), 6)
    return {
        "amps": scatter_about(seeds[0], (OP, K, PB), 1.0, 6.0, ((0, 512),)),
        "domains": picks_of(seeds[1], OP, NVB, K, 4096),
        "owner": draw_owner(jax.random.fold_in(seeds[5], 71), 0),
        "coupling": draw_coupling(jax.random.fold_in(seeds[5], 71), 0),
        "integrals": scatter_about(seeds[4], (NV, NV), (K * PB // 2) ** -0.5, 0.125, ((0, 16), (1, 32))),
    }


def reference(amps, domains, owner, coupling, integrals):
    slot_dom = domains[owner]
    slot_amps = amps[owner]
    blocks = jnp.arange(NVB, dtype=jnp.int32)
    onehot = slot_dom[:, :, None] == blocks[None, None, :]
    tile_full = jnp.einsum("pkc,pkx->pcx", onehot.astype(jnp.float32), slot_amps.astype(jnp.float32))
    tile_full = tile_full.astype(jnp.bfloat16).reshape(OP, NV)
    in_domain = jnp.any(onehot, axis=1).astype(jnp.float32)

    def one_block(target):
        keep_mask = coupling[:, target].astype(jnp.bfloat16)
        masked = (tile_full.reshape(OP, NVB, PB) * keep_mask[None, :, None]).reshape(OP, NV)
        column_block = lax.dynamic_slice_in_dim(integrals, target * PB, PB, 1)
        return jnp.dot(masked, column_block, preferred_element_type=jnp.float32)

    by_block = lax.map(one_block, blocks)
    result = jnp.transpose(by_block, (1, 0, 2)) * in_domain[:, :, None]
    return result.reshape(OP, NV)
```

```python
import functools

import jax
import jax.numpy as jnp
from jax import lax
from jax.experimental import pallas as pl
from jax.experimental.pallas import tpu as pltpu
from jax.sharding import PartitionSpec as P

HALF_Y = 2
STRIDE = 4


def contract(
    place, coupling, dom_rows, dom_cols, owner, near, up, down, far_a, far_b, integrals,
    out, act, rows_of, tiles, blocks, sem,
):
    target, residue, group = place[0], place[1], place[2]
    n_act, pairs, depth = tiles.shape
    chunk_slots = pairs // dom_rows.shape[0]
    width = dom_rows.shape[1]
    nvb = coupling.shape[0]

    def note(c, found):
        @pl.when(coupling[c, target] > 0)
        def _():
            act[found] = c
        return found + (coupling[c, target] > 0).astype(jnp.int32)

    lax.fori_loop(0, nvb, note, jnp.int32(0))

    def fetch(i):
        start = pl.multiple_of(act[i] * depth, depth)
        return pltpu.make_async_copy(integrals.at[pl.ds(start, depth), :], blocks.at[i], sem.at[i])

    for i in range(n_act):
        fetch(i).start()

    rows = n_act * chunk_slots
    row = lax.broadcasted_iota(jnp.int32, (rows, width), 0)
    lane = lax.broadcasted_iota(jnp.int32, (rows, width), 1)
    wanted = jnp.full((rows, width), -1, jnp.int32)
    for i in range(n_act):
        wanted = jnp.where(row // chunk_slots == i, act[i], wanted)
    wanted = jnp.where(lane // (width // chunk_slots) == row % chunk_slots, wanted, -1)
    rows_of[...] = wanted

    def expand(ref, offset, z):
        pick = (dom_rows[pl.ds(z, 1), :] == rows_of[...]).astype(jnp.float32).astype(jnp.bfloat16)
        got = jnp.dot(pick, ref[pl.ds(offset, width), :], preferred_element_type=jnp.float32)
        at = pl.ds(pl.multiple_of(z * chunk_slots, chunk_slots), chunk_slots)
        for i in range(n_act):
            tiles[i, at, :] = got[i * chunk_slots : (i + 1) * chunk_slots].astype(jnp.bfloat16)

    count = near.shape[0] // width
    for ref, step in ((near, 0), (up, 1), (down, STRIDE - 1)):
        at = lax.rem(residue + step, STRIDE)
        for j in range(count):
            expand(ref, j * width, j * STRIDE + at)
    at = lax.rem(residue + 2, STRIDE)
    for j in range(count):
        ref = far_a if j < count // 2 else far_b
        expand(ref, (j % (count // 2)) * width, j * STRIDE + at)

    own = owner[pl.ds(group, 1), :] - group * pairs
    own = jnp.transpose(jnp.broadcast_to(own, (pairs, pairs)))
    slot = lax.broadcasted_iota(jnp.int32, (pairs, pairs), 1)
    inside = jnp.max((dom_cols[...] == target).astype(jnp.float32), axis=0, keepdims=True)
    order = jnp.where(own == slot, jnp.broadcast_to(inside, (pairs, pairs)), 0.0)

    total = jnp.zeros(out.shape, jnp.float32)
    for i in range(n_act):
        fetch(i).wait()
        total = total + jnp.dot(tiles[i], blocks[i], preferred_element_type=jnp.float32)
    out[...] = jnp.dot(
        order, total, precision=lax.Precision.HIGHEST, preferred_element_type=jnp.float32
    )


def on_device(amps, domains, owner, coupling, integrals):
    n_blk, n_grp = lax.axis_size("blk"), lax.axis_size("grp")
    n_z = n_grp // HALF_Y
    me_blk = lax.axis_index("blk")
    me_z = lax.axis_index("grp") // HALF_Y
    depth, cols = integrals.shape
    nvb = coupling.shape[0]
    slots, k, _ = amps.shape
    pairs = slots * n_grp
    chunk = slots * HALF_Y

    whole = lax.all_gather(integrals, "blk", axis=0, tiled=True)

    couples = [[z * HALF_Y + y for y in range(HALF_Y)] for z in range(n_z)]
    strided = [
        [(i * STRIDE + q) * HALF_Y + y for i in range(n_z // STRIDE)]
        for q in range(STRIDE)
        for y in range(HALF_Y)
    ]
    above = [((g + HALF_Y) % n_grp, g) for g in range(n_grp)]
    below = [(g, (g + HALF_Y) % n_grp) for g in range(n_grp)]
    both = lax.all_gather(amps, "grp", axis=0, tiled=True, axis_index_groups=couples)
    near = lax.all_gather(both, "grp", axis=0, tiled=True, axis_index_groups=strided)
    near = near.reshape(near.shape[0] * k, depth)
    half = near.shape[0] // 2
    up = lax.ppermute(near, "grp", above)
    down = lax.ppermute(near, "grp", below)
    far_a = lax.ppermute(up[:half], "grp", above)
    far_b = lax.ppermute(down[half:], "grp", below)

    place = jnp.stack([me_z, me_z % STRIDE, me_blk]).astype(jnp.int32)
    mine = lax.dynamic_slice_in_dim(domains, me_blk * pairs, pairs)
    dom_rows = mine.reshape(n_z, chunk * k)
    dom_cols = domains.T
    n_act = nvb // 2
    vmem = pl.BlockSpec(memory_space=pltpu.VMEM)
    smem = pl.BlockSpec(memory_space=pltpu.SMEM)
    grid_spec = pltpu.PrefetchScalarGridSpec(
        num_scalar_prefetch=1,
        grid=(1,),
        in_specs=[
            smem,
            pl.BlockSpec((n_z, chunk * k), lambda i, p: (0, 0)),
            pl.BlockSpec((k, pairs), lambda i, p: (0, p[2])),
            pl.BlockSpec((n_blk, pairs), lambda i, p: (0, 0)),
            vmem, vmem, vmem, vmem, vmem,
            pl.BlockSpec(memory_space=pltpu.HBM),
        ],
        out_specs=vmem,
        scratch_shapes=[
            pltpu.SMEM((nvb,), jnp.int32),
            pltpu.VMEM((n_act * chunk, chunk * k), jnp.int32),
            pltpu.VMEM((n_act, pairs, depth), jnp.bfloat16),
            pltpu.VMEM((n_act, depth, cols), jnp.bfloat16),
            pltpu.SemaphoreType.DMA((n_act,)),
        ],
    )
    return pl.pallas_call(
        contract,
        grid_spec=grid_spec,
        out_shape=jax.ShapeDtypeStruct((pairs, cols), jnp.float32),
        compiler_params=pltpu.CompilerParams(vmem_limit_bytes=60 * 2**20),
    )(
        place, coupling, dom_rows, dom_cols, owner.reshape(n_blk, pairs),
        near, up, down, far_a, far_b, whole,
    )


def solution(mesh):
    return jax.shard_map(
        on_device,
        mesh=mesh,
        in_specs=(P(("blk", "grp"), None, None), P(), P(), P(), P("blk", "grp")),
        out_specs=P("blk", "grp"),
        check_vma=False,
    )
```

```python
import jax
import jax.numpy as jnp
from jax import lax
from jax.experimental import pallas as pl
from jax.experimental.pallas import tpu as pltpu
from jax.sharding import PartitionSpec as P


HALF_Y = 2
STRIDE = 4
HEAD = 4
HEAD_MIB = 48
MIB = 2**20


EARLY = ((0, 0, 0, 4), (0, 1, 0, 4), (1, 0, 0, 4), (3, 0, 0, 4), (2, 0, 0, 4))
LATE = ((3, 1, 0, 4), (1, 1, 0, 4), (2, 1, 0, 4))


def lines_of(place, doms, k):
    width = doms.shape[1]
    lane = lax.broadcasted_iota(jnp.int32, (width, width), 1)
    other = lax.broadcasted_iota(jnp.int32, (width, width), 0)
    same = (lane // k == other // k).astype(jnp.float32).astype(jnp.bfloat16)
    table = doms[...]
    inside = (table == place[0]).astype(jnp.float32).astype(jnp.bfloat16)
    hits = jnp.dot(inside, same, preferred_element_type=jnp.float32)
    return jnp.where(hits > 0, table, -2), lax.broadcasted_iota(jnp.int32, table.shape, 0)


def expand(kinds, place, doms, pieces, tiles):
    residue, half = place[1], place[3]
    n_act, count, _ = tiles.shape
    width = doms.shape[1]
    chunk = count * width // sum(p.shape[0] for p in pieces)
    k = width // chunk
    table, table_row = lines_of(place, doms, k)
    rows = n_act * chunk
    row = lax.broadcasted_iota(jnp.int32, (rows, width), 0)
    lane = lax.broadcasted_iota(jnp.int32, (rows, width), 1)
    wanted = jnp.full((rows, width), -1, jnp.int32)
    for i in range(n_act):
        wanted = jnp.where(row // chunk == i, place[HEAD + i], wanted)
    wanted = jnp.where(lane // k == row % chunk, wanted, -1)
    per = doms.shape[0] // (HALF_Y * STRIDE)
    at = 0
    for piece, (step, across, first, z_count) in zip(pieces, kinds):
        parts = piece.shape[0] // width
        base = ((half ^ across) * STRIDE + lax.rem(residue + step, STRIDE)) * per + first * parts // z_count
        for j in range(parts):
            line = jnp.max(jnp.where(table_row == base + j, table, -2), axis=0, keepdims=True)
            pick = (line == wanted).astype(jnp.float32).astype(jnp.bfloat16)
            got = jnp.dot(pick, piece[pl.ds(j * width, width), :], preferred_element_type=jnp.float32)
            for i in range(n_act):
                tiles[i, at : at + chunk, :] = got[i * chunk : (i + 1) * chunk].astype(jnp.bfloat16)
            at += chunk


def head_kernel(place, doms, *refs):
    pieces, (integrals, part, blocks, tiles, sem) = refs[: len(EARLY)], refs[len(EARLY) :]
    n_act, depth, _ = blocks.shape

    def fetch(i):
        start = pl.multiple_of(place[HEAD + i] * depth, depth)
        return pltpu.make_async_copy(integrals.at[pl.ds(start, depth), :], blocks.at[i], sem.at[i])

    for i in range(n_act):
        fetch(i).start()
    expand(EARLY, place, doms, pieces, tiles)
    total = jnp.zeros(part.shape, jnp.float32)
    for i in range(n_act):
        fetch(i).wait()
        total = total + jnp.dot(tiles[i], blocks[i], preferred_element_type=jnp.float32)
    part[...] = total


def finish_kernel(place, doms, owner, part, blocks, *refs):
    pieces, out, tiles = refs[:-2], refs[-2], refs[-1]
    residue, group, half = place[1], place[2], place[3]
    expand(LATE, place, doms, pieces, tiles)
    pairs = out.shape[0]
    per_z = pairs // sum(c for *_, c in EARLY + LATE)
    at = lax.broadcasted_iota(jnp.int32, (1, pairs), 1)
    slot = jnp.zeros((1, pairs), jnp.int32)
    low = 0
    for step, across, first, z_count in EARLY + LATE:
        inner = at - low
        z = (first + inner // per_z) * STRIDE + lax.rem(residue + step, STRIDE)
        here = (z * HALF_Y + (half ^ across)) * per_z + inner % per_z
        slot = jnp.where(at >= low, here, slot)
        low += z_count * per_z
    own = owner[pl.ds(group, 1), :] - group * pairs
    own = jnp.transpose(jnp.broadcast_to(own, (pairs, pairs)))
    order = (own == slot).astype(jnp.float32)
    total = jnp.zeros((tiles.shape[1], out.shape[1]), jnp.float32)
    for i in range(tiles.shape[0]):
        total = total + jnp.dot(tiles[i], blocks[i], preferred_element_type=jnp.float32)
    out[...] = jnp.dot(
        order,
        jnp.concatenate([part[...], total], axis=0),
        precision=lax.Precision.HIGHEST,
        preferred_element_type=jnp.float32,
    )


def on_device(amps, domains, owner, coupling, integrals):
    n_blk, n_grp = lax.axis_size("blk"), lax.axis_size("grp")
    n_z = n_grp // HALF_Y
    me_blk, me_grp = lax.axis_index("blk"), lax.axis_index("grp")
    me_z = me_grp // HALF_Y
    depth, cols = integrals.shape
    nvb = coupling.shape[0]
    n_act = nvb // 2
    slots, k, _ = amps.shape
    pairs = slots * n_grp

    whole = lax.all_gather(integrals, "blk", axis=0, tiled=True)

    strided = [
        [(i * STRIDE + q) * HALF_Y + y for i in range(n_z // STRIDE)]
        for q in range(STRIDE)
        for y in range(HALF_Y)
    ]

    def send(x, hops):
        return lax.ppermute(x, "grp", [(g, (g + hops * HALF_Y) % n_grp) for g in range(n_grp)])

    near = lax.all_gather(amps, "grp", axis=0, tiled=True, axis_index_groups=strided)
    near = near.reshape(near.shape[0] * k, depth)
    near_x = lax.ppermute(near, "grp", [(g, g ^ 1) for g in range(n_grp)])
    up = send(near, -1)
    down = send(near, 1)

    keep = lax.dynamic_index_in_dim(coupling, me_z, axis=1, keepdims=False) > 0
    numbers = jnp.arange(nvb, dtype=jnp.int32)
    before = jnp.sum((numbers[None, :] < numbers[:, None]) & keep[None, :], axis=1)
    chosen = keep[None, :] & (before[None, :] == jnp.arange(n_act)[:, None])
    act = jnp.sum(jnp.where(chosen, numbers[None, :], 0), axis=1)
    head = jnp.stack([me_z, me_z % STRIDE, me_blk, me_grp % HALF_Y])
    place = jnp.concatenate([head, act]).astype(jnp.int32)
    mine = lax.dynamic_slice_in_dim(domains, me_blk * pairs, pairs)
    mine = mine.reshape(n_z // STRIDE, STRIDE, HALF_Y, slots * k)
    doms = jnp.transpose(mine, (2, 1, 0, 3)).reshape(-1, 2 * slots * k)
    owners = owner.reshape(n_blk, pairs)
    ready, place, doms, owners = lax.optimization_barrier((up, place, doms, owners))
    far = send(ready, -1)
    down_x = send(near_x, 1)
    up_x = send(near_x, -1)
    far_x = send(down_x, 1)
    vmem = pl.BlockSpec(memory_space=pltpu.VMEM)
    smem = pl.BlockSpec(memory_space=pltpu.SMEM)

    def cost(flops):
        return pl.CostEstimate(flops=flops, bytes_accessed=2 * MIB, transcendentals=0)

    pieces = (near, near_x, up, down, far)
    rows = sum(p.shape[0] for p in pieces) // k
    part, blocks = pl.pallas_call(
        head_kernel,
        in_specs=[smem] + [vmem] * (1 + len(pieces)) + [pl.BlockSpec(memory_space=pl.ANY)],
        out_specs=(vmem, vmem),
        out_shape=(
            jax.ShapeDtypeStruct((rows, cols), jnp.float32),
            jax.ShapeDtypeStruct((n_act, depth, cols), jnp.bfloat16),
        ),
        scratch_shapes=[
            pltpu.VMEM((n_act, rows, depth), jnp.bfloat16),
            pltpu.SemaphoreType.DMA((n_act,)),
        ],
        compiler_params=pltpu.CompilerParams(vmem_limit_bytes=HEAD_MIB * MIB),
        cost_estimate=cost(2**29),
    )(place, doms, *pieces, whole)
    pieces = (down_x, up_x, far_x)
    return pl.pallas_call(
        finish_kernel,
        in_specs=[smem] + [vmem] * (4 + len(pieces)),
        out_specs=vmem,
        out_shape=jax.ShapeDtypeStruct((pairs, cols), jnp.float32),
        scratch_shapes=[pltpu.VMEM((n_act, pairs - rows, depth), jnp.bfloat16)],
        compiler_params=pltpu.CompilerParams(vmem_limit_bytes=16 * MIB),
        cost_estimate=cost(2**29),
    )(place, doms, owners, part, blocks, *pieces)


def solution(mesh):
    return jax.shard_map(
        on_device,
        mesh=mesh,
        in_specs=(P(("blk", "grp"), None, None), P(), P(), P(), P("blk", "grp")),
        out_specs=P("blk", "grp"),
        check_vma=False,
    )
```

```python
import jax
import jax.numpy as jnp
from jax import lax
from jax.experimental import pallas as pl
from jax.experimental.pallas import tpu as pltpu
from jax.sharding import PartitionSpec as P


HALF_Y = 2
STRIDE = 4
HEAD = 4
HEAD_MIB = 48
MIB = 2**20


EARLY = ((0, 0), (0, 1), (1, 0), (3, 0), (2, 0), (3, 1), (1, 1))
LATE = ((2, 1),)


def picks_of(kinds, place, doms, n_act, k):
    residue, half = place[1], place[3]
    width = doms.shape[1]
    chunk = width // k
    lane = lax.broadcasted_iota(jnp.int32, (width, width), 1)
    other = lax.broadcasted_iota(jnp.int32, (width, width), 0)
    same = (lane // k == other // k).astype(jnp.float32).astype(jnp.bfloat16)
    table = doms[...]
    inside = (table == place[0]).astype(jnp.float32).astype(jnp.bfloat16)
    hits = jnp.dot(inside, same, preferred_element_type=jnp.float32)
    table = jnp.where(hits > 0, table, -2)
    table_row = lax.broadcasted_iota(jnp.int32, table.shape, 0)
    rows = n_act * chunk
    row = lax.broadcasted_iota(jnp.int32, (rows, width), 0)
    lane = lax.broadcasted_iota(jnp.int32, (rows, width), 1)
    wanted = jnp.full((rows, width), -1, jnp.int32)
    for i in range(n_act):
        wanted = jnp.where(row // chunk == i, place[HEAD + i], wanted)
    wanted = jnp.where(lane // k == row % chunk, wanted, -1)
    per = doms.shape[0] // (HALF_Y * STRIDE)
    picks = []
    for step, across in kinds:
        base = ((half ^ across) * STRIDE + lax.rem(residue + step, STRIDE)) * per
        for j in range(per):
            line = jnp.max(jnp.where(table_row == base + j, table, -2), axis=0, keepdims=True)
            picks.append((line == wanted).astype(jnp.float32).astype(jnp.bfloat16))
    return picks


def expand(picks, pieces, tiles):
    n_act, count, _ = tiles.shape
    chunk = count // len(picks)
    width = picks[0].shape[1]
    per = len(picks) // len(pieces)
    for n, pick in enumerate(picks):
        piece = pieces[n // per][pl.ds(n % per * width, width), :]
        got = jnp.dot(pick, piece, preferred_element_type=jnp.float32)
        for i in range(n_act):
            tiles[i, n * chunk : (n + 1) * chunk, :] = got[i * chunk : (i + 1) * chunk].astype(jnp.bfloat16)


def order_of(kinds, own, place, per_z):
    residue, half = place[1], place[3]
    share = STRIDE * per_z
    shape = (own.shape[0], len(kinds) * share)
    at = lax.broadcasted_iota(jnp.int32, (1, shape[1]), 1)
    slot = jnp.zeros((1, shape[1]), jnp.int32)
    for n, (step, across) in enumerate(kinds):
        inner = at - n * share
        z = inner // per_z * STRIDE + lax.rem(residue + step, STRIDE)
        slot = jnp.where(inner >= 0, (z * HALF_Y + (half ^ across)) * per_z + inner % per_z, slot)
    return (own[:, : shape[1]] == slot).astype(jnp.float32)


def reorder(order, rows):
    return jnp.dot(order, rows, precision=lax.Precision.HIGHEST, preferred_element_type=jnp.float32)


def head_kernel(place, doms, owner, *refs):
    pieces = refs[: len(EARLY)]
    integrals, part, blocks, late_picks, late_order, tiles, sem = refs[len(EARLY) :]
    n_act, depth, _ = blocks.shape

    def fetch(i):
        start = pl.multiple_of(place[HEAD + i] * depth, depth)
        return pltpu.make_async_copy(integrals.at[pl.ds(start, depth), :], blocks.at[i], sem.at[i])

    for i in range(n_act):
        fetch(i).start()
    pairs = part.shape[0]
    per_z = tiles.shape[1] // (len(EARLY) * STRIDE)
    k = doms.shape[0] * doms.shape[1] // pairs
    picks = picks_of(EARLY + LATE, place, doms, n_act, k)
    n_late = late_picks.shape[0]
    for n, pick in enumerate(picks[-n_late:]):
        late_picks[n] = pick
    expand(picks[:-n_late], pieces, tiles)
    own = owner[pl.ds(place[2], 1), :] - place[2] * pairs
    own = jnp.transpose(jnp.broadcast_to(own, (pairs, pairs)))
    late_order[...] = order_of(LATE, own, place, per_z)
    order = order_of(EARLY, own, place, per_z)
    total = jnp.zeros((tiles.shape[1], part.shape[1]), jnp.float32)
    for i in range(n_act):
        fetch(i).wait()
        total = total + jnp.dot(tiles[i], blocks[i], preferred_element_type=jnp.float32)
    part[...] = reorder(order, total)


def finish_kernel(part, blocks, late_picks, late_order, *refs):
    pieces, (out, tiles) = refs[: len(LATE)], refs[len(LATE) :]
    expand([late_picks[n] for n in range(late_picks.shape[0])], pieces, tiles)
    total = jnp.zeros((tiles.shape[1], out.shape[1]), jnp.float32)
    for i in range(tiles.shape[0]):
        total = total + jnp.dot(tiles[i], blocks[i], preferred_element_type=jnp.float32)
    out[...] = part[...] + reorder(late_order[...], total)


def on_device(amps, domains, owner, coupling, integrals):
    n_blk, n_grp = lax.axis_size("blk"), lax.axis_size("grp")
    n_z = n_grp // HALF_Y
    me_blk, me_grp = lax.axis_index("blk"), lax.axis_index("grp")
    me_z = me_grp // HALF_Y
    depth, cols = integrals.shape
    nvb = coupling.shape[0]
    n_act = nvb // 2
    slots, k, _ = amps.shape
    pairs = slots * n_grp

    whole = lax.all_gather(integrals, "blk", axis=0, tiled=True)

    strided = [
        [(i * STRIDE + q) * HALF_Y + y for i in range(n_z // STRIDE)]
        for q in range(STRIDE)
        for y in range(HALF_Y)
    ]

    def send(x, hops):
        return lax.ppermute(x, "grp", [(g, (g + hops * HALF_Y) % n_grp) for g in range(n_grp)])

    near = lax.all_gather(amps, "grp", axis=0, tiled=True, axis_index_groups=strided)
    near = near.reshape(near.shape[0] * k, depth)
    near_x = lax.ppermute(near, "grp", [(g, g ^ 1) for g in range(n_grp)])
    up = send(near, -1)
    down = send(near, 1)

    keep = lax.dynamic_index_in_dim(coupling, me_z, axis=1, keepdims=False) > 0
    numbers = jnp.arange(nvb, dtype=jnp.int32)
    before = jnp.sum((numbers[None, :] < numbers[:, None]) & keep[None, :], axis=1)
    chosen = keep[None, :] & (before[None, :] == jnp.arange(n_act)[:, None])
    act = jnp.sum(jnp.where(chosen, numbers[None, :], 0), axis=1)
    head = jnp.stack([me_z, me_z % STRIDE, me_blk, me_grp % HALF_Y])
    place = jnp.concatenate([head, act]).astype(jnp.int32)
    mine = lax.dynamic_slice_in_dim(domains, me_blk * pairs, pairs)
    mine = mine.reshape(n_z // STRIDE, STRIDE, HALF_Y, slots * k)
    doms = jnp.transpose(mine, (2, 1, 0, 3)).reshape(-1, 2 * slots * k)
    owners = owner.reshape(n_blk, pairs)
    ready, place, doms, owners = lax.optimization_barrier((up, place, doms, owners))
    far = send(ready, -1)
    down_x = send(near_x, 1)
    up_x = send(near_x, -1)
    far_x = lax.ppermute(far, "grp", [(g, g ^ 1) for g in range(n_grp)])
    vmem = pl.BlockSpec(memory_space=pltpu.VMEM)
    smem = pl.BlockSpec(memory_space=pltpu.SMEM)

    def cost(flops):
        return pl.CostEstimate(flops=flops, bytes_accessed=2 * MIB, transcendentals=0)

    early, late = (near, near_x, up, down, far, down_x, up_x), (far_x,)
    n_early, n_late = (sum(p.shape[0] for p in ps) // k for ps in (early, late))
    chunk = doms.shape[1] // k
    prepared = (
        jax.ShapeDtypeStruct((pairs, cols), jnp.float32),
        jax.ShapeDtypeStruct((n_act, depth, cols), jnp.bfloat16),
        jax.ShapeDtypeStruct((n_late // chunk, n_act * chunk, doms.shape[1]), jnp.bfloat16),
        jax.ShapeDtypeStruct((pairs, n_late), jnp.float32),
    )
    prepared = pl.pallas_call(
        head_kernel,
        in_specs=[smem] + [vmem] * (2 + len(early)) + [pl.BlockSpec(memory_space=pl.ANY)],
        out_specs=(vmem,) * len(prepared),
        out_shape=prepared,
        scratch_shapes=[
            pltpu.VMEM((n_act, n_early, depth), jnp.bfloat16),
            pltpu.SemaphoreType.DMA((n_act,)),
        ],
        compiler_params=pltpu.CompilerParams(vmem_limit_bytes=HEAD_MIB * MIB),
        cost_estimate=cost(2**29),
    )(place, doms, owners, *early, whole)
    return pl.pallas_call(
        finish_kernel,
        in_specs=[vmem] * (len(prepared) + len(late)),
        out_specs=vmem,
        out_shape=jax.ShapeDtypeStruct((pairs, cols), jnp.float32),
        scratch_shapes=[pltpu.VMEM((n_act, n_late, depth), jnp.bfloat16)],
        compiler_params=pltpu.CompilerParams(vmem_limit_bytes=16 * MIB),
        cost_estimate=cost(2**27),
    )(*prepared, *late)


def solution(mesh):
    return jax.shard_map(
        on_device,
        mesh=mesh,
        in_specs=(P(("blk", "grp"), None, None), P(), P(), P(), P("blk", "grp")),
        out_specs=P("blk", "grp"),
        check_vma=False,
    )
```

```python
import jax
import jax.numpy as jnp
from jax import lax
from jax.experimental import pallas as pl
from jax.experimental.pallas import tpu as pltpu
from jax.sharding import PartitionSpec as P


HALF_Y = 2
STRIDE = 4
HEAD = 4
HEAD_MIB = 48
MIB = 2**20


EARLY = ((0, 0), (0, 1), (1, 0), (3, 0), (2, 0), (3, 1), (1, 1))
LATE = ((2, 1),)


def picks_of(kinds, place, doms, n_act, k):
    residue, half = place[1], place[3]
    width = doms.shape[1]
    chunk = width // k
    lane = lax.broadcasted_iota(jnp.int32, (width, width), 1)
    other = lax.broadcasted_iota(jnp.int32, (width, width), 0)
    same = (lane // k == other // k).astype(jnp.float32).astype(jnp.bfloat16)
    table = doms[...]
    inside = (table == place[0]).astype(jnp.float32).astype(jnp.bfloat16)
    hits = jnp.dot(inside, same, preferred_element_type=jnp.float32)
    table = jnp.where(hits > 0, table, -2)
    table_row = lax.broadcasted_iota(jnp.int32, table.shape, 0)
    rows = n_act * chunk
    row = lax.broadcasted_iota(jnp.int32, (rows, width), 0)
    lane = lax.broadcasted_iota(jnp.int32, (rows, width), 1)
    wanted = jnp.full((rows, width), -1, jnp.int32)
    for i in range(n_act):
        wanted = jnp.where(row // chunk == i, place[HEAD + i], wanted)
    wanted = jnp.where(lane // k == row % chunk, wanted, -1)
    per = doms.shape[0] // (HALF_Y * STRIDE)
    picks = []
    for step, across in kinds:
        base = ((half ^ across) * STRIDE + lax.rem(residue + step, STRIDE)) * per
        for j in range(per):
            line = jnp.max(jnp.where(table_row == base + j, table, -2), axis=0, keepdims=True)
            picks.append((line == wanted).astype(jnp.float32).astype(jnp.bfloat16))
    return picks


def expand(picks, pieces, tiles):
    n_act, count, _ = tiles.shape
    chunk = count // len(picks)
    width = picks[0].shape[1]
    per = len(picks) // len(pieces)
    for n, pick in enumerate(picks):
        piece = pieces[n // per][pl.ds(n % per * width, width), :]
        got = jnp.dot(pick, piece, preferred_element_type=jnp.float32)
        for i in range(n_act):
            tiles[i, n * chunk : (n + 1) * chunk, :] = got[i * chunk : (i + 1) * chunk].astype(jnp.bfloat16)


def order_of(kinds, own, place, per_z):
    residue, half = place[1], place[3]
    share = STRIDE * per_z
    shape = (own.shape[0], len(kinds) * share)
    at = lax.broadcasted_iota(jnp.int32, (1, shape[1]), 1)
    slot = jnp.zeros((1, shape[1]), jnp.int32)
    for n, (step, across) in enumerate(kinds):
        inner = at - n * share
        z = inner // per_z * STRIDE + lax.rem(residue + step, STRIDE)
        slot = jnp.where(inner >= 0, (z * HALF_Y + (half ^ across)) * per_z + inner % per_z, slot)
    return (own[:, : shape[1]] == slot).astype(jnp.float32).astype(jnp.bfloat16)


def reorder(order, rows):
    parts = []
    for _ in range(3):
        part = rows.astype(jnp.bfloat16)
        rows = rows - part.astype(jnp.float32)
        parts.append(part)
    return jnp.dot(
        jnp.concatenate([order] * 3, axis=1),
        jnp.concatenate(parts, axis=0),
        preferred_element_type=jnp.float32,
    )


def head_kernel(place, doms, owner, *refs):
    pieces = refs[: len(EARLY)]
    integrals, part, blocks, late_picks, late_order, tiles, sem = refs[len(EARLY) :]
    n_act, depth, _ = blocks.shape

    def fetch(i):
        start = pl.multiple_of(place[HEAD + i] * depth, depth)
        return pltpu.make_async_copy(integrals.at[pl.ds(start, depth), :], blocks.at[i], sem.at[i])

    for i in range(n_act):
        fetch(i).start()
    pairs = part.shape[0]
    per_z = tiles.shape[1] // (len(EARLY) * STRIDE)
    k = doms.shape[0] * doms.shape[1] // pairs
    picks = picks_of(EARLY + LATE, place, doms, n_act, k)
    n_late = late_picks.shape[0]
    for n, pick in enumerate(picks[-n_late:]):
        late_picks[n] = pick
    expand(picks[:-n_late], pieces, tiles)
    own = owner[pl.ds(place[2], 1), :] - place[2] * pairs
    own = jnp.transpose(jnp.broadcast_to(own, (pairs, pairs)))
    late_order[...] = order_of(LATE, own, place, per_z)
    order = order_of(EARLY, own, place, per_z)
    total = jnp.zeros((tiles.shape[1], part.shape[1]), jnp.float32)
    for i in range(n_act):
        fetch(i).wait()
        total = total + jnp.dot(tiles[i], blocks[i], preferred_element_type=jnp.float32)
    part[...] = reorder(order, total)


def finish_kernel(part, blocks, late_picks, late_order, *refs):
    pieces, (out, tiles) = refs[: len(LATE)], refs[len(LATE) :]
    expand([late_picks[n] for n in range(late_picks.shape[0])], pieces, tiles)
    total = jnp.zeros((tiles.shape[1], out.shape[1]), jnp.float32)
    for i in range(tiles.shape[0]):
        total = total + jnp.dot(tiles[i], blocks[i], preferred_element_type=jnp.float32)
    out[...] = part[...] + reorder(late_order[...], total)


def on_device(amps, domains, owner, coupling, integrals):
    n_blk, n_grp = lax.axis_size("blk"), lax.axis_size("grp")
    n_z = n_grp // HALF_Y
    me_blk, me_grp = lax.axis_index("blk"), lax.axis_index("grp")
    me_z = me_grp // HALF_Y
    depth, cols = integrals.shape
    nvb = coupling.shape[0]
    n_act = nvb // 2
    slots, k, _ = amps.shape
    pairs = slots * n_grp

    whole = lax.all_gather(integrals, "blk", axis=0, tiled=True)

    strided = [
        [(i * STRIDE + q) * HALF_Y + y for i in range(n_z // STRIDE)]
        for q in range(STRIDE)
        for y in range(HALF_Y)
    ]

    def send(x, hops):
        return lax.ppermute(x, "grp", [(g, (g + hops * HALF_Y) % n_grp) for g in range(n_grp)])

    near = lax.all_gather(amps, "grp", axis=0, tiled=True, axis_index_groups=strided)
    near = near.reshape(near.shape[0] * k, depth)
    near_x = lax.ppermute(near, "grp", [(g, g ^ 1) for g in range(n_grp)])
    up = send(near, -1)
    down = send(near, 1)

    keep = lax.dynamic_index_in_dim(coupling, me_z, axis=1, keepdims=False) > 0
    numbers = jnp.arange(nvb, dtype=jnp.int32)
    before = jnp.sum((numbers[None, :] < numbers[:, None]) & keep[None, :], axis=1)
    chosen = keep[None, :] & (before[None, :] == jnp.arange(n_act)[:, None])
    act = jnp.sum(jnp.where(chosen, numbers[None, :], 0), axis=1)
    head = jnp.stack([me_z, me_z % STRIDE, me_blk, me_grp % HALF_Y])
    place = jnp.concatenate([head, act]).astype(jnp.int32)
    mine = lax.dynamic_slice_in_dim(domains, me_blk * pairs, pairs)
    mine = mine.reshape(n_z // STRIDE, STRIDE, HALF_Y, slots * k)
    doms = jnp.transpose(mine, (2, 1, 0, 3)).reshape(-1, 2 * slots * k)
    owners = owner.reshape(n_blk, pairs)
    ready, place, doms, owners = lax.optimization_barrier((up, place, doms, owners))
    far = send(ready, -1)
    down_x = send(near_x, 1)
    up_x = send(near_x, -1)
    far_x = lax.ppermute(far, "grp", [(g, g ^ 1) for g in range(n_grp)])
    vmem = pl.BlockSpec(memory_space=pltpu.VMEM)
    smem = pl.BlockSpec(memory_space=pltpu.SMEM)

    def cost(flops):
        return pl.CostEstimate(flops=flops, bytes_accessed=2 * MIB, transcendentals=0)

    early, late = (near, near_x, up, down, far, down_x, up_x), (far_x,)
    n_early, n_late = (sum(p.shape[0] for p in ps) // k for ps in (early, late))
    chunk = doms.shape[1] // k
    prepared = (
        jax.ShapeDtypeStruct((pairs, cols), jnp.float32),
        jax.ShapeDtypeStruct((n_act, depth, cols), jnp.bfloat16),
        jax.ShapeDtypeStruct((n_late // chunk, n_act * chunk, doms.shape[1]), jnp.bfloat16),
        jax.ShapeDtypeStruct((pairs, n_late), jnp.bfloat16),
    )
    prepared = pl.pallas_call(
        head_kernel,
        in_specs=[smem] + [vmem] * (2 + len(early)) + [pl.BlockSpec(memory_space=pl.ANY)],
        out_specs=(vmem,) * len(prepared),
        out_shape=prepared,
        scratch_shapes=[
            pltpu.VMEM((n_act, n_early, depth), jnp.bfloat16),
            pltpu.SemaphoreType.DMA((n_act,)),
        ],
        compiler_params=pltpu.CompilerParams(vmem_limit_bytes=HEAD_MIB * MIB),
        cost_estimate=cost(2**29),
    )(place, doms, owners, *early, whole)
    return pl.pallas_call(
        finish_kernel,
        in_specs=[vmem] * (len(prepared) + len(late)),
        out_specs=vmem,
        out_shape=jax.ShapeDtypeStruct((pairs, cols), jnp.float32),
        scratch_shapes=[pltpu.VMEM((n_act, n_late, depth), jnp.bfloat16)],
        compiler_params=pltpu.CompilerParams(vmem_limit_bytes=16 * MIB),
        cost_estimate=cost(2**27),
    )(*prepared, *late)


def solution(mesh):
    return jax.shard_map(
        on_device,
        mesh=mesh,
        in_specs=(P(("blk", "grp"), None, None), P(), P(), P(), P("blk", "grp")),
        out_specs=P("blk", "grp"),
        check_vma=False,
    )
```

```python
import jax
import jax.numpy as jnp
from jax import lax
from jax.experimental import pallas as pl
from jax.experimental.pallas import tpu as pltpu
from jax.sharding import PartitionSpec as P


HALF_Y = 2
STRIDE = 4
HEAD = 4
HEAD_MIB = 48
MIB = 2**20


FIRST = ((0, 0), (0, 1), (1, 0), (3, 0), (2, 0))
EARLY = FIRST + ((3, 1), (1, 1))
LATE = ((2, 1),)


def picks_of(kinds, place, doms, n_act, k):
    residue, half = place[1], place[3]
    width = doms.shape[1]
    chunk = width // k
    lane = lax.broadcasted_iota(jnp.int32, (width, width), 1)
    other = lax.broadcasted_iota(jnp.int32, (width, width), 0)
    same = (lane // k == other // k).astype(jnp.float32).astype(jnp.bfloat16)
    table = doms[...]
    inside = (table == place[0]).astype(jnp.float32).astype(jnp.bfloat16)
    hits = jnp.dot(inside, same, preferred_element_type=jnp.float32)
    table = jnp.where(hits > 0, table, -2)
    table_row = lax.broadcasted_iota(jnp.int32, table.shape, 0)
    rows = n_act * chunk
    row = lax.broadcasted_iota(jnp.int32, (rows, width), 0)
    lane = lax.broadcasted_iota(jnp.int32, (rows, width), 1)
    wanted = jnp.full((rows, width), -1, jnp.int32)
    for i in range(n_act):
        wanted = jnp.where(row // chunk == i, place[HEAD + i], wanted)
    wanted = jnp.where(lane // k == row % chunk, wanted, -1)
    per = doms.shape[0] // (HALF_Y * STRIDE)
    picks = []
    for step, across in kinds:
        base = ((half ^ across) * STRIDE + lax.rem(residue + step, STRIDE)) * per
        for j in range(per):
            line = jnp.max(jnp.where(table_row == base + j, table, -2), axis=0, keepdims=True)
            picks.append((line == wanted).astype(jnp.float32).astype(jnp.bfloat16))
    return picks


def expand(picks, pieces, tiles):
    n_act, count, _ = tiles.shape
    chunk = count // len(picks)
    width = picks[0].shape[1]
    per = len(picks) // len(pieces)
    for n, pick in enumerate(picks):
        piece = pieces[n // per][pl.ds(n % per * width, width), :]
        got = jnp.dot(pick, piece, preferred_element_type=jnp.float32)
        for i in range(n_act):
            tiles[i, n * chunk : (n + 1) * chunk, :] = got[i * chunk : (i + 1) * chunk].astype(jnp.bfloat16)


def order_of(kinds, own, place, per_z):
    residue, half = place[1], place[3]
    share = STRIDE * per_z
    shape = (own.shape[0], len(kinds) * share)
    at = lax.broadcasted_iota(jnp.int32, (1, shape[1]), 1)
    slot = jnp.zeros((1, shape[1]), jnp.int32)
    for n, (step, across) in enumerate(kinds):
        inner = at - n * share
        z = inner // per_z * STRIDE + lax.rem(residue + step, STRIDE)
        slot = jnp.where(inner >= 0, (z * HALF_Y + (half ^ across)) * per_z + inner % per_z, slot)
    return (own[:, : shape[1]] == slot).astype(jnp.float32).astype(jnp.bfloat16)


def reorder(order, rows):
    parts = []
    for _ in range(3):
        part = rows.astype(jnp.bfloat16)
        rows = rows - part.astype(jnp.float32)
        parts.append(part)
    return jnp.dot(
        jnp.concatenate([order] * 3, axis=1),
        jnp.concatenate(parts, axis=0),
        preferred_element_type=jnp.float32,
    )


def pick_kernel(place, doms, owner, *refs):
    pieces, tiles = refs[:-1], refs[-1]
    k = pieces[0].shape[0] * len(pieces) // tiles.shape[1]
    n_act = tiles.shape[0] - 1
    expand(picks_of(FIRST, place, doms, n_act, k), pieces, tiles.at[:n_act])
    pairs = owner.shape[1]
    own = owner[pl.ds(place[2], 1), :] - place[2] * pairs
    own = jnp.transpose(jnp.broadcast_to(own, (pairs, pairs)))
    order = order_of(EARLY + LATE, own, place, tiles.shape[1] // (len(FIRST) * STRIDE))
    half = pairs // 2
    tiles[n_act, :half, :pairs] = order[:half]
    tiles[n_act, :half, pairs:] = order[half:]


def head_kernel(place, doms, first, *refs):
    n_next = len(EARLY) - len(FIRST)
    pieces, (integrals, part, blocks, late_picks, late_order, tiles, sem) = refs[:n_next], refs[n_next:]
    n_act, depth, _ = blocks.shape

    def fetch(i):
        start = pl.multiple_of(place[HEAD + i] * depth, depth)
        return pltpu.make_async_copy(integrals.at[pl.ds(start, depth), :], blocks.at[i], sem.at[i])

    for i in range(n_act):
        fetch(i).start()
    pairs = part.shape[0]
    k = doms.shape[0] * doms.shape[1] // pairs
    picks = picks_of(EARLY[len(FIRST) :] + LATE, place, doms, n_act, k)
    n_late = late_picks.shape[0]
    for n, pick in enumerate(picks[-n_late:]):
        late_picks[n] = pick
    expand(picks[:-n_late], pieces, tiles)
    slab = first[n_act, : pairs // 2, :]
    order = jnp.concatenate([slab[:, :pairs], slab[:, pairs:]], axis=0)
    n_early = pairs - late_order.shape[1]
    late_order[...] = order[:, n_early:]
    order = order[:, :n_early]
    above = jnp.zeros((first.shape[1], part.shape[1]), jnp.float32)
    below = jnp.zeros((tiles.shape[1], part.shape[1]), jnp.float32)
    for i in range(n_act):
        fetch(i).wait()
        above = above + jnp.dot(first[i], blocks[i], preferred_element_type=jnp.float32)
        below = below + jnp.dot(tiles[i], blocks[i], preferred_element_type=jnp.float32)
    part[...] = reorder(order, jnp.concatenate([above, below], axis=0))


def finish_kernel(part, blocks, late_picks, late_order, *refs):
    pieces, (out, tiles) = refs[: len(LATE)], refs[len(LATE) :]
    expand([late_picks[n] for n in range(late_picks.shape[0])], pieces, tiles)
    total = jnp.zeros((tiles.shape[1], out.shape[1]), jnp.float32)
    for i in range(tiles.shape[0]):
        total = total + jnp.dot(tiles[i], blocks[i], preferred_element_type=jnp.float32)
    out[...] = part[...] + reorder(late_order[...], total)


def on_device(amps, domains, owner, coupling, integrals):
    n_blk, n_grp = lax.axis_size("blk"), lax.axis_size("grp")
    n_z = n_grp // HALF_Y
    me_blk, me_grp = lax.axis_index("blk"), lax.axis_index("grp")
    me_z = me_grp // HALF_Y
    depth, cols = integrals.shape
    nvb = coupling.shape[0]
    n_act = nvb // 2
    slots, k, _ = amps.shape
    pairs = slots * n_grp

    whole = lax.all_gather(integrals, "blk", axis=0, tiled=True)

    strided = [
        [(i * STRIDE + q) * HALF_Y + y for i in range(n_z // STRIDE)]
        for q in range(STRIDE)
        for y in range(HALF_Y)
    ]

    def send(x, hops):
        return lax.ppermute(x, "grp", [(g, (g + hops * HALF_Y) % n_grp) for g in range(n_grp)])

    near = lax.all_gather(amps, "grp", axis=0, tiled=True, axis_index_groups=strided)
    near = near.reshape(near.shape[0] * k, depth)
    near_x = lax.ppermute(near, "grp", [(g, g ^ 1) for g in range(n_grp)])
    up = send(near, -1)
    down = send(near, 1)

    keep = lax.dynamic_index_in_dim(coupling, me_z, axis=1, keepdims=False) > 0
    numbers = jnp.arange(nvb, dtype=jnp.int32)
    before = jnp.sum((numbers[None, :] < numbers[:, None]) & keep[None, :], axis=1)
    chosen = keep[None, :] & (before[None, :] == jnp.arange(n_act)[:, None])
    act = jnp.sum(jnp.where(chosen, numbers[None, :], 0), axis=1)
    head = jnp.stack([me_z, me_z % STRIDE, me_blk, me_grp % HALF_Y])
    place = jnp.concatenate([head, act]).astype(jnp.int32)
    mine = lax.dynamic_slice_in_dim(domains, me_blk * pairs, pairs)
    mine = mine.reshape(n_z // STRIDE, STRIDE, HALF_Y, slots * k)
    doms = jnp.transpose(mine, (2, 1, 0, 3)).reshape(-1, 2 * slots * k)
    owners = owner.reshape(n_blk, pairs)
    ready, place, doms, owners = lax.optimization_barrier((up, place, doms, owners))
    far = send(ready, -1)
    down_x = send(near_x, 1)
    up_x = send(near_x, -1)
    far_x = lax.ppermute(far, "grp", [(g, g ^ 1) for g in range(n_grp)])
    vmem = pl.BlockSpec(memory_space=pltpu.VMEM)
    smem = pl.BlockSpec(memory_space=pltpu.SMEM)

    def cost(flops):
        return pl.CostEstimate(flops=flops, bytes_accessed=2 * MIB, transcendentals=0)

    early, late = (near, near_x, up, down, far, down_x, up_x), (far_x,)
    n_early, n_late = (sum(p.shape[0] for p in ps) // k for ps in (early, late))
    chunk = doms.shape[1] // k
    prepared = (
        jax.ShapeDtypeStruct((pairs, cols), jnp.float32),
        jax.ShapeDtypeStruct((n_act, depth, cols), jnp.bfloat16),
        jax.ShapeDtypeStruct((n_late // chunk, n_act * chunk, doms.shape[1]), jnp.bfloat16),
        jax.ShapeDtypeStruct((pairs, n_late), jnp.bfloat16),
    )
    first = early[: len(FIRST)]
    n_first = sum(p.shape[0] for p in first) // k
    tiles = pl.pallas_call(
        pick_kernel,
        in_specs=[smem] + [vmem] * (2 + len(first)),
        out_specs=vmem,
        out_shape=jax.ShapeDtypeStruct((n_act + 1, n_first, depth), jnp.bfloat16),
        compiler_params=pltpu.CompilerParams(vmem_limit_bytes=8 * MIB),
        cost_estimate=cost(2**28),
    )(place, doms, owners, *first)
    prepared = pl.pallas_call(
        head_kernel,
        in_specs=[smem] + [vmem] * (2 + len(early) - len(FIRST)) + [pl.BlockSpec(memory_space=pl.ANY)],
        out_specs=(vmem,) * len(prepared),
        out_shape=prepared,
        scratch_shapes=[pltpu.VMEM((n_act, n_early - n_first, depth), jnp.bfloat16), pltpu.SemaphoreType.DMA((n_act,))],
        compiler_params=pltpu.CompilerParams(vmem_limit_bytes=HEAD_MIB * MIB),
        cost_estimate=cost(2**29),
    )(place, doms, tiles, *early[len(FIRST) :], whole)
    return pl.pallas_call(
        finish_kernel,
        in_specs=[vmem] * (len(prepared) + len(late)),
        out_specs=vmem,
        out_shape=jax.ShapeDtypeStruct((pairs, cols), jnp.float32),
        scratch_shapes=[pltpu.VMEM((n_act, n_late, depth), jnp.bfloat16)],
        compiler_params=pltpu.CompilerParams(vmem_limit_bytes=16 * MIB),
        cost_estimate=cost(2**27),
    )(*prepared, *late)


def solution(mesh):
    return jax.shard_map(
        on_device,
        mesh=mesh,
        in_specs=(P(("blk", "grp"), None, None), P(), P(), P(), P("blk", "grp")),
        out_specs=P("blk", "grp"),
        check_vma=False,
    )
```
